32 devices in a mesh: space: 8 (over z, x), lag: 4 (over y, core).
Axes of the slice: x: 2, y: 2, z: 4, core: 2. Of those that a mesh axis runs over, the one named last changes fastest.
Arguments:
- prior: bfloat16 [8, 4, 64, 1024], P('lag', None, None, 'space'), may hold values from -6 to 6
- obs_value: float32 [8192], P('space'), may hold values from -6 to 6
- obs_weight: float32 [8192], P('space'), may hold values from 0.5 to 4
- obs_coef: float32 [4, 8192], P(None, 'space'), may hold values from 0.1 to 1
- obs_column: int32 [8192], P('space'), may hold values from 0 to 127
- obs_count: int32 [8], P('space'), may hold values from 512 to 1024
- halo_lists: int32 [2, 4096], P(None, 'space'), may hold values from 0 to 1023
- neighbours: int32 [64, 1024], P(None, 'space'), may hold values from 0 to 2047
- localization: float32 [64, 1024], P(None, 'space'), may hold values from 0.05 to 1
Outputs:
- analysis: bfloat16 [8, 4, 64, 1024], P('lag', None, None, 'space')
The draws below stay inside these ranges and needn't reach their ends.
Inputs may be any that keep to these rules, and one draw needn't show every extreme that they name: `obs_column`: each observation's column within its own tile. `obs_count`: slots at or beyond a tile's count hold no observation. `halo_lists`: slot numbers within the sending tile. `neighbours`: positions in the extended list of the column's tile.
All inputs are finite; a program needn't handle non-finite values.
Results may differ from the reference program's by a relative error of at most 0.0062.
Values may be sent and summed in bfloat16 or wider, within the bound.
A program may use at most 64 MiB of HBM per device.

```python
import math
import jax
import jax.numpy as jnp
from jax import lax

K = 64
SPEC = 4
NB = 64
NSI = 2
COLS_DEV = 128
OBS_DEV = 1024
HALO = 512
TILES = 8
COLS = 1024
OBS = 8192
LAGS = 8


def place_ends(entries, own_key, smallest, high):
    spot = [jax.random.randint(jax.random.fold_in(own_key, axis), (), 0, length) for axis, length in enumerate(entries.shape)]
    widest = entries.shape.index(max(entries.shape))
    beside = spot[:widest] + [(spot[widest] + 1) % entries.shape[widest]] + spot[widest + 1:]
    return entries.at[tuple(spot)].set(smallest).at[tuple(beside)].set(high)


def block_scale(stream_key, extent, split, least, high):
    factor_of, own = 1.0, jax.random.fold_in(stream_key, 6)
    for axis_at, blocks in split:
        draws = jnp.exp(jax.random.uniform(jax.random.fold_in(own, axis_at), (blocks,), jnp.float32, least / len(split), high / len(split)))
        factor_of = factor_of * jnp.repeat(draws, extent[axis_at] // blocks).reshape([-1 if axis == axis_at else 1 for axis in range(len(extent))])
    return factor_of


def centred(rng, shape, scale, most, split=(), kind=jnp.bfloat16):
    level = block_scale(rng, shape, split, -0.22, 0.18) if split else 1.0
    drawn = jax.random.normal(rng, shape, jnp.float32) * scale * level
    return jnp.minimum(jnp.maximum(drawn, -most), most).astype(kind)


def setup_inputs(seed: int = 0) -> dict:
    streams_of = jax.random.split(jax.random.key(seed), 10)
    return {
        "prior": centred(streams_of[0], (LAGS, SPEC, K, COLS), 1.0, 6.0, ((0, 4), (3, 8))),
        "obs_value": centred(streams_of[1], (OBS,), 1.0, 6.0, ((0, 8),), jnp.float32),
        "obs_weight": jnp.clip(jnp.exp(math.log(4.0) - 2.0794415 * jax.random.uniform(streams_of[2], (OBS,), jnp.float32) ** block_scale(streams_of[2], (OBS,), ((0, 8),), -0.2, 0.2)), 0.5, 4.0),
        "obs_coef": jnp.clip(jnp.exp(math.log(1.0) - 2.3025851 * jax.random.uniform(streams_of[3], (SPEC, OBS), jnp.float32) ** block_scale(streams_of[3], (SPEC, OBS), ((1, 8),), -0.2, 0.2)), 0.1, 1.0),
        "obs_column": place_ends(jax.random.randint(streams_of[4], (OBS,), 0, COLS_DEV), jax.random.fold_in(streams_of[4], 1), 0, COLS_DEV - 1).astype(jnp.int32),
        "obs_count": place_ends(jax.random.randint(streams_of[5], (TILES,), HALO, OBS_DEV + 1), jax.random.fold_in(streams_of[5], 1), HALO, OBS_DEV).astype(jnp.int32),
        "halo_lists": place_ends(jax.random.randint(streams_of[6], (2, OBS // 2), 0, OBS_DEV), jax.random.fold_in(streams_of[6], 1), 0, OBS_DEV - 1).astype(jnp.int32),
        "neighbours": place_ends(jax.random.randint(streams_of[7], (NB, COLS), 0, OBS_DEV + 2 * HALO), jax.random.fold_in(streams_of[7], 1), 0, (OBS_DEV + 2 * HALO) - 1).astype(jnp.int32),
        "localization": jnp.clip(0.05 + 0.95 * jax.random.uniform(streams_of[8], (NB, COLS), jnp.float32) ** block_scale(streams_of[8], (NB, COLS), ((1, 8),), -0.2, 0.2), 0.05, 1.0),
    }


def matmul(left, right):
    return jnp.einsum('ikc,kjc->ijc', left, right, precision=lax.Precision.HIGHEST)

def observe(newest, coef, column, value, weight, count):
    picked = jnp.take(newest, column, axis=2).astype(jnp.float32)
    hx = lax.optimization_barrier(jnp.sum(coef[:, None, :] * picked, axis=0))
    mean_hx = lax.optimization_barrier(jnp.mean(hx, axis=0))
    valid = (jnp.arange(OBS_DEV) < count).astype(jnp.float32)
    pert = ((hx - mean_hx[None, :]) * valid[None, :]).astype(jnp.bfloat16)
    info = jnp.stack([weight * valid, (value - mean_hx) * valid]).astype(jnp.bfloat16)
    return (pert, info)

def solve(inputs):
    ext_pert, ext_info, table, local_weight = inputs
    gathered = jnp.take(ext_pert, table, axis=1)
    ginfo = jnp.take(ext_info, table, axis=1).astype(jnp.float32)
    weighted = (gathered.astype(jnp.float32) * (local_weight * ginfo[0])[None]).astype(jnp.bfloat16)
    gram = jnp.einsum('inc,jnc->ijc', gathered.astype(jnp.float32), weighted.astype(jnp.float32), precision=lax.Precision.HIGHEST)
    drive = jnp.einsum('inc,nc->ic', weighted.astype(jnp.float32), ginfo[1], precision=lax.Precision.HIGHEST)
    eye = jnp.eye(K, dtype=jnp.float32)[:, :, None]
    matrix = eye + gram / (K - 1)
    scale = jnp.sqrt(lax.optimization_barrier(jnp.sum(matrix * matrix, axis=(0, 1))))
    ycur = matrix / scale[None, None, :]
    zcur = jnp.broadcast_to(eye, matrix.shape)
    for step in range(NSI):
        smat = 1.5 * eye - 0.5 * matmul(zcur, ycur)
        ycur = matmul(ycur, smat)
        zcur = matmul(smat, zcur)
    inverse = matmul(zcur, zcur) / scale[None, None, :]
    mean_weight = jnp.einsum('ijc,jc->ic', inverse, drive, precision=lax.Precision.HIGHEST) / (K - 1)
    root = zcur / jnp.sqrt(scale)[None, None, :]
    return (root + mean_weight[:, None, :]).astype(jnp.bfloat16)

def reference(prior, obs_value, obs_weight, obs_coef, obs_column, obs_count, halo_lists, neighbours, localization):
    tiles = TILES
    newest = prior[LAGS - 1].reshape(SPEC, K, tiles, COLS_DEV).transpose(2, 0, 1, 3)
    coef = obs_coef.reshape(SPEC, tiles, OBS_DEV).transpose(1, 0, 2)
    pert, info = jax.vmap(observe)(newest, coef, obs_column.reshape(tiles, OBS_DEV), obs_value.reshape(tiles, OBS_DEV), obs_weight.reshape(tiles, OBS_DEV), obs_count)
    lists = halo_lists.reshape(2, tiles, HALO)
    pick = jax.vmap(lambda arr, idx: jnp.take(arr, idx, axis=1))
    up_pert, up_info = (pick(pert, lists[0]), pick(info, lists[0]))
    down_pert, down_info = (pick(pert, lists[1]), pick(info, lists[1]))
    zero_pert = jnp.zeros_like(up_pert[:1])
    zero_info = jnp.zeros_like(up_info[:1])
    below_pert = jnp.concatenate([zero_pert, up_pert[:-1]], axis=0)
    below_info = jnp.concatenate([zero_info, up_info[:-1]], axis=0)
    above_pert = jnp.concatenate([down_pert[1:], zero_pert], axis=0)
    above_info = jnp.concatenate([down_info[1:], zero_info], axis=0)
    ext_pert = jnp.concatenate([pert, below_pert, above_pert], axis=2)
    ext_info = jnp.concatenate([info, below_info, above_info], axis=2)
    table = neighbours.reshape(NB, tiles, COLS_DEV).transpose(1, 0, 2)
    local_weight = localization.reshape(NB, tiles, COLS_DEV).transpose(1, 0, 2)
    trans = lax.map(solve, (ext_pert, ext_info, table, local_weight))
    trans = trans.transpose(1, 2, 0, 3).reshape(K, K, COLS)
    values = prior.astype(jnp.float32)
    prior_mean = lax.optimization_barrier(jnp.mean(values, axis=2, keepdims=True))
    prior_pert = (values - prior_mean).astype(jnp.bfloat16)
    mixed = jnp.einsum('lskc,kjc->lsjc', prior_pert.astype(jnp.float32), trans.astype(jnp.float32), precision=lax.Precision.HIGHEST)
    return (prior_mean + mixed).astype(jnp.bfloat16)
```

```python
import functools

import jax
import jax.numpy as jnp
from jax import lax
from jax.experimental import pallas as pl
from jax.experimental.pallas import tpu as pltpu
from jax.sharding import PartitionSpec as P

MESH = pl.DeviceIdType.MESH
F32 = jnp.float32
BF16 = jnp.bfloat16
PACK = 4
VMEM = pl.BlockSpec(memory_space=pltpu.VMEM)
ANY = pl.BlockSpec(memory_space=pl.ANY)
SMEM = pl.BlockSpec(memory_space=pltpu.SMEM)


def iota(shape, dim):
    return lax.broadcasted_iota(jnp.int32, shape, dim)


def onehot(row, depth):
    return jnp.where(row == iota((depth, row.shape[1]), 0), 1.0, 0.0).astype(BF16)


def dot(a, b):
    return jnp.dot(a, b, preferred_element_type=F32)


def split(x):
    high = x.astype(BF16)
    return high, (x - high.astype(F32)).astype(BF16)


def columns_kernel(prior_ref, send_ref, turned):
    windows, species, members, cols = prior_ref.shape
    rows = windows * species
    for r in range(rows):
        x = prior_ref[r // species, r % species].astype(F32)
        turned[r * cols : (r + 1) * cols, :] = jnp.concatenate([x, x], axis=0).T
    low = iota((rows, 2 * members), 1) < members
    share = cols // send_ref.shape[0]
    for c in range(0, cols, 2):
        even = turned[pl.ds(c, rows, stride=cols), :]
        odd = turned[pl.ds(c + 1, rows, stride=cols), :]
        at = (c % share) * members
        send_ref[c // share, :, at : at + 2 * members] = jnp.where(low, even, odd).astype(BF16)


def restore_kernel(got_ref, out_ref, turned):
    windows, species, members, cols = out_ref.shape
    rows = windows * species
    share = cols // got_ref.shape[0]
    for c in range(0, cols, 2):
        at = (c % share) * members
        x = got_ref[c // share, :, at : at + 2 * members].astype(F32)
        turned[pl.ds(c, rows, stride=cols), :] = x
        turned[pl.ds(c + 1, rows, stride=cols), :] = pltpu.roll(x, members, 1)
    for r in range(rows):
        x = turned[r * cols : (r + 1) * cols, :].T
        out_ref[r // species, r % species] = x[:members].astype(BF16)


def greet_lag(lags, me):
    barrier = pltpu.get_barrier_semaphore()
    for d in range(1, lags):
        pl.semaphore_signal(barrier, inc=1, device_id={"lag": lax.rem(me + d, lags)}, device_id_type=MESH)
    pl.semaphore_wait(barrier, lags - 1)


def swap(lags, me, send_ref, got_ref, send_sem, recv_sem):
    copies = []
    for d in range(1, lags):
        peer = lax.rem(me + d, lags)
        copies.append(
            pltpu.make_async_remote_copy(
                src_ref=send_ref.at[peer],
                dst_ref=got_ref.at[me],
                send_sem=send_sem.at[d - 1],
                recv_sem=recv_sem.at[d - 1],
                device_id={"lag": peer},
                device_id_type=MESH,
            )
        )
    return copies


def open_kernel(lags, prior_ref, send_ref, newest_ref, got_ref, ssem, rsem, nssem, nrsem, lsem):
    me = lax.axis_index("lag")
    holder = lags - 1
    last = prior_ref.shape[0] - 1
    greet_lag(lags, me)

    def spread(d):
        return pltpu.make_async_remote_copy(
            src_ref=prior_ref.at[last],
            dst_ref=newest_ref,
            send_sem=nssem.at[d],
            recv_sem=nrsem,
            device_id={"lag": lax.rem(me + d + 1, lags)},
            device_id_type=MESH,
        )

    mine = pltpu.make_async_copy(send_ref.at[me], got_ref.at[me], lsem.at[0])
    own = pltpu.make_async_copy(prior_ref.at[last], newest_ref, lsem.at[1])

    @pl.when(me == holder)
    def _():
        for d in range(lags - 1):
            spread(d).start()
        own.start()

    mine.start()
    copies = swap(lags, me, send_ref, got_ref, ssem, rsem)
    for copy in copies:
        copy.start()
    for copy in copies:
        copy.wait()
    mine.wait()

    @pl.when(me == holder)
    def _():
        for d in range(lags - 1):
            spread(d).wait_send()
        own.wait()

    @pl.when(me != holder)
    def _():
        spread(0).wait_recv()


def close_kernel(lags, send_ref, got_ref, ssem, rsem, lsem):
    me = lax.axis_index("lag")
    greet_lag(lags, me)
    mine = pltpu.make_async_copy(send_ref.at[me], got_ref.at[me], lsem)
    copies = swap(lags, me, send_ref, got_ref, ssem, rsem)
    for copy in copies:
        copy.start()
    mine.start()
    for copy in copies:
        copy.wait()
    mine.wait()


def observe_kernel(newest_ref, coef_ref, column_ref, value_ref, weight_ref, count_ref, lists_ref, feat_ref, halo_ref):
    species, members, cols = newest_ref.shape
    slots = column_ref.shape[1]
    pick = onehot(column_ref[...], cols)
    hx = coef_ref[0:1, :] * dot(newest_ref[0], pick)
    for s in range(1, species):
        hx = hx + coef_ref[s : s + 1, :] * dot(newest_ref[s], pick)
    mean = jnp.sum(hx, axis=0, keepdims=True) / members
    valid = jnp.where(iota((1, slots), 1) < count_ref[0], 1.0, 0.0)
    feat_ref[:members] = ((hx - mean) * valid).astype(BF16)
    extra = feat_ref.shape[0] - members
    row = iota((extra, slots), 0)
    info0 = weight_ref[...] * valid
    info1 = (value_ref[...] - mean) * valid
    feat_ref[members:] = jnp.where(row == 0, info0, jnp.where(row == 1, info1, 0.0)).astype(BF16)
    feat = feat_ref[...]
    for r in range(2):
        halo_ref[r] = dot(feat, onehot(lists_ref[r : r + 1, :], slots)).astype(BF16)


def halo_kernel(tiles, halo_ref, got_ref, ssem, rsem):
    t = lax.axis_index("space")
    barrier = pltpu.get_barrier_semaphore()
    below, above = t > 0, t < tiles - 1
    up, down = jnp.minimum(t + 1, tiles - 1), jnp.maximum(t - 1, 0)

    @pl.when(above)
    def _():
        pl.semaphore_signal(barrier, inc=1, device_id={"space": up}, device_id_type=MESH)

    @pl.when(below)
    def _():
        pl.semaphore_signal(barrier, inc=1, device_id={"space": down}, device_id_type=MESH)

    @pl.when(below & above)
    def _():
        pl.semaphore_wait(barrier, 2)

    @pl.when(below != above)
    def _():
        pl.semaphore_wait(barrier, 1)

    def move(r, to):
        return pltpu.make_async_remote_copy(
            src_ref=halo_ref.at[r],
            dst_ref=got_ref.at[r],
            send_sem=ssem.at[r],
            recv_sem=rsem.at[r],
            device_id={"space": to},
            device_id_type=MESH,
        )

    @pl.when(above)
    def _():
        move(0, up).start()

    @pl.when(below)
    def _():
        move(1, down).start()

    @pl.when(above)
    def _():
        move(0, up).wait_send()
        move(1, up).wait_recv()

    @pl.when(below)
    def _():
        move(1, down).wait_send()
        move(0, down).wait_recv()


def solve_kernel(tiles, lags, feat_ref, halo_ref, table_ref, local_ref, prior_ref, out_ref, ext, tabs, locs):
    t, me = lax.axis_index("space"), lax.axis_index("lag")
    near, cols = table_ref.shape
    rows = prior_ref.shape[1]
    slots, halo = feat_ref.shape[1], halo_ref.shape[2]
    share = cols // lags
    members = prior_ref.shape[2] // share
    groups = share // PACK
    wide = PACK * members
    depth = slots + 2 * halo

    ext[:, :slots] = feat_ref[...]
    ext[:, slots : slots + halo] = jnp.where(t > 0, halo_ref[0].astype(F32), 0.0).astype(BF16)
    ext[:, slots + halo :] = jnp.where(t < tiles - 1, halo_ref[1].astype(F32), 0.0).astype(BF16)
    x = table_ref[...].astype(F32)
    tabs[...] = jnp.concatenate([x, x], axis=0).T
    x = local_ref[...]
    locs[...] = jnp.concatenate([x, x], axis=0).T

    start = pl.multiple_of(me * share, share)
    low = iota((1, 2 * near), 1) < near

    def row_of(ref, q):
        parts = []
        for m in range(0, PACK, 2):
            c = start + q * PACK + m
            parts.append(jnp.where(low, ref[pl.ds(c, 1), :], ref[pl.ds(c + 1, 1), :]))
        return jnp.concatenate(parts, axis=1)

    lane = iota((members, wide), 1)
    masks = [jnp.where(lane // members == m, 1.0, 0.0).astype(BF16) for m in range(PACK)]
    ones = jnp.concatenate(masks, axis=0)
    eye = jnp.where(lane % members == iota((members, wide), 0), 1.0, 0.0)

    def diag(x):
        return jnp.concatenate([x * mask for mask in masks], axis=0)

    qs = range(groups)
    table = [row_of(tabs, q).astype(jnp.int32) for q in qs]
    local = [row_of(locs, q) for q in qs]
    source = ext[...]
    picked = [dot(source, onehot(table[q], depth)) for q in qs]
    gathered = [picked[q][:members] for q in qs]
    weighted = [(gathered[q] * (local[q] * picked[q][members : members + 1])).astype(BF16) for q in qs]
    gram = [
        lax.dot_general(
            gathered[q].astype(BF16), diag(weighted[q]), (((1,), (1,)), ((), ())), preferred_element_type=F32
        )
        for q in qs
    ]
    matrix = [eye + gram[q] / (members - 1) for q in qs]
    total = [jnp.sum(matrix[q] * matrix[q], axis=0, keepdims=True) for q in qs]

    def group_sum(x):
        high, low_part = split(x)
        mid, last = split(x - high.astype(F32))
        count = x.shape[0]
        y = dot(jnp.concatenate([high.astype(F32), mid.astype(F32), last.astype(F32)], axis=0).astype(BF16), ones)
        return y[:count] + y[count : 2 * count] + y[2 * count :]

    scale2 = group_sum(jnp.concatenate(total, axis=0))
    root = lax.rsqrt(scale2)
    inv = [root[q : q + 1] for q in qs]
    a = [matrix[q] * inv[q] for q in qs]
    ab = [a[q].astype(BF16) for q in qs]
    p = [dot(ab[q], diag(ab[q])) for q in qs]
    pb = [p[q].astype(BF16) for q in qs]
    z = [
        2.25 * eye
        - 2.4375 * a[q]
        + 1.6875 * p[q]
        + dot((0.0625 * p[q] - 0.5625 * a[q]).astype(BF16), diag(pb[q]))
        for q in qs
    ]
    zs = [jnp.concatenate(split(z[q]), axis=0) for q in qs]

    def apply(q, x):
        high, small = split(x)
        y = dot(zs[q], diag(high))
        return y[:members] + y[members:] + dot(zs[q][:members], diag(small))

    drive = []
    for q in qs:
        x = weighted[q].astype(F32) * picked[q][members + 1 : members + 2]
        y = dot(jnp.concatenate(split(x), axis=0), ones)
        drive.append(y[:members] + y[members:])
    u = [apply(q, drive[q]) for q in qs]
    mean_weight = [apply(q, u[q]) for q in qs]
    for q in qs:
        trans = (z[q] * jnp.sqrt(inv[q]) + mean_weight[q] * (inv[q] / (members - 1))).astype(BF16)
        prior = jnp.concatenate([prior_ref[l, :, q * wide : (q + 1) * wide].astype(F32) for l in range(lags)], axis=0)
        mean = dot(prior.astype(BF16), ones) / members
        mixed = mean + dot((prior - mean).astype(BF16), diag(trans))
        for l in range(lags):
            out_ref[l, :, q * wide : (q + 1) * wide] = mixed[l * rows : (l + 1) * rows].astype(BF16)


def body(prior, obs_value, obs_weight, obs_coef, obs_column, obs_count, halo_lists, neighbours, localization):
    lags, tiles = lax.axis_size("lag"), lax.axis_size("space")
    windows, species, members, cols = prior.shape
    slots, halo, near = obs_column.shape[0], halo_lists.shape[1], neighbours.shape[0]
    share = cols // lags
    rows = windows * species
    block = jax.ShapeDtypeStruct((lags, rows, share * members), BF16)
    feats = members + 16
    turned = pltpu.VMEM((rows * cols, 2 * members), F32)

    send = pl.pallas_call(
        columns_kernel, out_shape=block, in_specs=[VMEM], out_specs=VMEM, scratch_shapes=[turned], name="columns"
    )(prior)
    newest, windows_all = pl.pallas_call(
        functools.partial(open_kernel, lags),
        out_shape=(jax.ShapeDtypeStruct((species, members, cols), BF16), block),
        in_specs=[ANY, ANY],
        out_specs=(ANY, ANY),
        scratch_shapes=[
            pltpu.SemaphoreType.DMA((lags - 1,)),
            pltpu.SemaphoreType.DMA((lags - 1,)),
            pltpu.SemaphoreType.DMA((lags - 1,)),
            pltpu.SemaphoreType.DMA,
            pltpu.SemaphoreType.DMA((2,)),
        ],
        compiler_params=pltpu.CompilerParams(collective_id=0, has_side_effects=True),
        name="open",
    )(prior, send)
    feat, listed = pl.pallas_call(
        observe_kernel,
        out_shape=(jax.ShapeDtypeStruct((feats, slots), BF16), jax.ShapeDtypeStruct((2, feats, halo), BF16)),
        in_specs=[VMEM, VMEM, VMEM, VMEM, VMEM, SMEM, VMEM],
        out_specs=(VMEM, VMEM),
        name="observe",
    )(
        newest,
        obs_coef,
        obs_column.reshape(1, slots),
        obs_value.reshape(1, slots),
        obs_weight.reshape(1, slots),
        obs_count,
        halo_lists,
    )
    around = pl.pallas_call(
        functools.partial(halo_kernel, tiles),
        out_shape=jax.ShapeDtypeStruct((2, feats, halo), BF16),
        in_specs=[ANY],
        out_specs=ANY,
        scratch_shapes=[pltpu.SemaphoreType.DMA((2,)), pltpu.SemaphoreType.DMA((2,))],
        compiler_params=pltpu.CompilerParams(collective_id=1, has_side_effects=True),
        name="halo",
    )(listed)
    mixed = pl.pallas_call(
        functools.partial(solve_kernel, tiles, lags),
        out_shape=block,
        in_specs=[VMEM] * 5,
        out_specs=VMEM,
        scratch_shapes=[
            pltpu.VMEM((feats, slots + 2 * halo), BF16),
            pltpu.VMEM((cols, 2 * near), F32),
            pltpu.VMEM((cols, 2 * near), F32),
        ],
        name="solve",
    )(feat, around, neighbours, localization, windows_all)
    back = pl.pallas_call(
        functools.partial(close_kernel, lags),
        out_shape=block,
        in_specs=[ANY],
        out_specs=ANY,
        scratch_shapes=[
            pltpu.SemaphoreType.DMA((lags - 1,)),
            pltpu.SemaphoreType.DMA((lags - 1,)),
            pltpu.SemaphoreType.DMA,
        ],
        compiler_params=pltpu.CompilerParams(collective_id=2, has_side_effects=True),
        name="close",
    )(mixed)
    return pl.pallas_call(
        restore_kernel,
        out_shape=jax.ShapeDtypeStruct(prior.shape, BF16),
        in_specs=[VMEM],
        out_specs=VMEM,
        scratch_shapes=[turned],
        name="restore",
    )(back)


def solution(mesh):
    return jax.shard_map(
        body,
        mesh=mesh,
        in_specs=(
            P("lag", None, None, "space"),
            P("space"),
            P("space"),
            P(None, "space"),
            P("space"),
            P("space"),
            P(None, "space"),
            P(None, "space"),
            P(None, "space"),
        ),
        out_specs=P("lag", None, None, "space"),
        check_vma=False,
    )
```

```python
import functools

import jax
import jax.numpy as jnp
from jax import lax
from jax.experimental import pallas as pl
from jax.experimental.pallas import tpu as pltpu
from jax.sharding import PartitionSpec as P

MESH = pl.DeviceIdType.MESH
F32 = jnp.float32
BF16 = jnp.bfloat16
PACK = 4
VMEM = pl.BlockSpec(memory_space=pltpu.VMEM)
ANY = pl.BlockSpec(memory_space=pl.ANY)
SMEM = pl.BlockSpec(memory_space=pltpu.SMEM)


def iota(shape, dim):
    return lax.broadcasted_iota(jnp.int32, shape, dim)


def onehot(row, depth):
    return jnp.where(row == iota((depth, row.shape[1]), 0), 1.0, 0.0).astype(BF16)


def dot(a, b):
    return jnp.dot(a, b, preferred_element_type=F32)


def split(x):
    high = x.astype(BF16)
    return high, (x - high.astype(F32)).astype(BF16)


def remote(src, dst, send_sem, recv_sem, where):
    return pltpu.make_async_remote_copy(
        src_ref=src, dst_ref=dst, send_sem=send_sem, recv_sem=recv_sem, device_id=where, device_id_type=MESH
    )


def kernel(
    tiles,
    lags,
    count_ref,
    prior_ref,
    value_ref,
    weight_ref,
    coef_ref,
    column_ref,
    lists_ref,
    table_ref,
    local_ref,
    out_ref,
    prior_v,
    value_v,
    weight_v,
    coef_v,
    column_v,
    lists_v,
    table_v,
    local_v,
    newest,
    turned,
    send,
    got,
    back,
    home,
    feat_v,
    listed,
    around,
    pick_v,
    list_v,
    near_v,
    tabs,
    locs,
    in_sem,
    new_send,
    new_recv,
    swap_send,
    swap_recv,
    halo_send,
    halo_recv,
    back_send,
    back_recv,
    self_sem,
):
    t, me = lax.axis_index("space"), lax.axis_index("lag")
    windows, species, members, cols = prior_v.shape
    rows = windows * species
    share = cols // lags
    slots, halo = column_v.shape[1], lists_v.shape[1]
    near = table_v.shape[0]
    holder = lags - 1
    below, above = t > 0, t < tiles - 1
    up, down = jnp.minimum(t + 1, tiles - 1), jnp.maximum(t - 1, 0)
    peers = [lax.rem(me + d, lags) for d in range(1, lags)]

    barrier = pltpu.get_barrier_semaphore()
    for peer in peers:
        pl.semaphore_signal(barrier, inc=1, device_id={"lag": peer}, device_id_type=MESH)

    @pl.when(above)
    def _():
        pl.semaphore_signal(barrier, inc=1, device_id={"space": up}, device_id_type=MESH)

    @pl.when(below)
    def _():
        pl.semaphore_signal(barrier, inc=1, device_id={"space": down}, device_id_type=MESH)

    pairs = [
        (prior_ref, prior_v),
        (column_ref, column_v),
        (lists_ref, lists_v),
        (coef_ref, coef_v),
        (value_ref, value_v),
        (weight_ref, weight_v),
        (table_ref, table_v),
        (local_ref, local_v),
    ]
    loads = [pltpu.make_async_copy(src, dst, in_sem.at[i]) for i, (src, dst) in enumerate(pairs)]
    for load in loads:
        load.start()

    @pl.when(below & above)
    def _():
        pl.semaphore_wait(barrier, lags + 1)

    @pl.when(below != above)
    def _():
        pl.semaphore_wait(barrier, lags)

    def spread(d):
        return remote(prior_ref.at[windows - 1], newest, new_send.at[d], new_recv, {"lag": peers[d]})

    own = pltpu.make_async_copy(prior_ref.at[windows - 1], newest, self_sem.at[0])

    @pl.when(me == holder)
    def _():
        for d in range(lags - 1):
            spread(d).start()
        own.start()

    loads[0].wait()
    for r in range(rows):
        x = prior_v[r // species, r % species].astype(F32)
        turned[r * cols : (r + 1) * cols, :] = jnp.concatenate([x, x], axis=0).T
    low = iota((1, 2 * members), 1) < members
    for c in range(0, cols, 2):
        even = turned[pl.ds(c, rows, stride=cols), :]
        odd = turned[pl.ds(c + 1, rows, stride=cols), :]
        at = (c % share) * members
        send[c // share, :, at : at + 2 * members] = jnp.where(low, even, odd).astype(BF16)
    for load in loads[1:]:
        load.wait()
    pick_v[...] = onehot(column_v[...], cols)
    for r in range(2):
        list_v[r] = onehot(lists_v[r : r + 1, :], slots)

    @pl.when(me == holder)
    def _():
        own.wait()

    @pl.when(me != holder)
    def _():
        spread(0).wait_recv()

    pick = pick_v[...]
    hx = coef_v[0:1, :] * dot(newest[0], pick)
    for s in range(1, species):
        hx = hx + coef_v[s : s + 1, :] * dot(newest[s], pick)
    mean = jnp.sum(hx, axis=0, keepdims=True) / members
    valid = jnp.where(iota((1, slots), 1) < count_ref[0], 1.0, 0.0)
    feat_v[:members] = ((hx - mean) * valid).astype(BF16)
    extra = feat_v.shape[0] - members
    row = iota((extra, slots), 0)
    info0 = weight_v[...] * valid
    info1 = (value_v[...] - mean) * valid
    feat_v[members:] = jnp.where(row == 0, info0, jnp.where(row == 1, info1, 0.0)).astype(BF16)
    feat = feat_v[...]
    for r in range(2):
        listed[r] = dot(feat, list_v[r]).astype(BF16)

    def move(r, to):
        return remote(listed.at[r], around.at[r], halo_send.at[r], halo_recv.at[r], {"space": to})

    @pl.when(above)
    def _():
        move(0, up).start()

    @pl.when(below)
    def _():
        move(1, down).start()

    @pl.when(t == 0)
    def _():
        around[0] = jnp.zeros(around.shape[1:], BF16)

    @pl.when(t == tiles - 1)
    def _():
        around[1] = jnp.zeros(around.shape[1:], BF16)

    mine = pltpu.make_async_copy(send.at[me], got.at[me], self_sem.at[1])
    mine.start()
    swaps = [
        remote(send.at[peer], got.at[me], swap_send.at[d], swap_recv.at[d], {"lag": peer})
        for d, peer in enumerate(peers)
    ]
    for copy in swaps:
        copy.start()

    x = table_v[...].astype(F32)
    tabs[...] = jnp.concatenate([x, x], axis=0).T
    x = local_v[...]
    locs[...] = jnp.concatenate([x, x], axis=0).T
    start = pl.multiple_of(me * share, share)
    low = iota((1, 2 * near), 1) < near
    groups = share // PACK
    wide = PACK * members
    qs = range(groups)

    def row_of(ref, q):
        parts = []
        for m in range(0, PACK, 2):
            c = start + q * PACK + m
            parts.append(jnp.where(low, ref[pl.ds(c, 1), :], ref[pl.ds(c + 1, 1), :]))
        return jnp.concatenate(parts, axis=1)

    lane = iota((members, wide), 1)
    masks = [jnp.where(lane // members == m, 1.0, 0.0).astype(BF16) for m in range(PACK)]
    ones = jnp.concatenate(masks, axis=0)
    eye = jnp.where(lane % members == iota((members, wide), 0), 1.0, 0.0)

    def diag(x):
        return jnp.concatenate([x * mask for mask in masks], axis=0)

    local = [row_of(locs, q) for q in qs]
    inner = []
    for q in qs:
        table = row_of(tabs, q).astype(jnp.int32)
        inner.append(dot(feat, onehot(table, slots)))
        near_v[q] = onehot(table - slots, 2 * halo)

    @pl.when(above)
    def _():
        move(0, up).wait_send()
        move(1, up).wait_recv()

    @pl.when(below)
    def _():
        move(1, down).wait_send()
        move(0, down).wait_recv()

    picked = [
        inner[q] + dot(around[0], near_v[q, :halo]) + dot(around[1], near_v[q, halo:]) for q in qs
    ]
    gathered = [picked[q][:members] for q in qs]
    weighted = [(gathered[q] * (local[q] * picked[q][members : members + 1])).astype(BF16) for q in qs]
    gram = [
        lax.dot_general(
            gathered[q].astype(BF16), diag(weighted[q]), (((1,), (1,)), ((), ())), preferred_element_type=F32
        )
        for q in qs
    ]
    matrix = [eye + gram[q] / (members - 1) for q in qs]
    total = [jnp.sum(matrix[q] * matrix[q], axis=0, keepdims=True) for q in qs]

    def group_sum(x):
        high, _ = split(x)
        mid, last = split(x - high.astype(F32))
        count = x.shape[0]
        y = dot(jnp.concatenate([high.astype(F32), mid.astype(F32), last.astype(F32)], axis=0).astype(BF16), ones)
        return y[:count] + y[count : 2 * count] + y[2 * count :]

    root = lax.rsqrt(group_sum(jnp.concatenate(total, axis=0)))
    inv = [root[q : q + 1] for q in qs]
    a = [matrix[q] * inv[q] for q in qs]
    ab = [a[q].astype(BF16) for q in qs]
    p = [dot(ab[q], diag(ab[q])) for q in qs]
    z = [
        2.25 * eye
        - 2.4375 * a[q]
        + 1.6875 * p[q]
        + dot((0.0625 * p[q] - 0.5625 * a[q]).astype(BF16), diag(p[q].astype(BF16)))
        for q in qs
    ]
    zs = [jnp.concatenate(split(z[q]), axis=0) for q in qs]

    def apply(q, x):
        high, small = split(x)
        y = dot(zs[q], diag(high))
        return y[:members] + y[members:] + dot(zs[q][:members], diag(small))

    drive = []
    for q in qs:
        x = weighted[q].astype(F32) * picked[q][members + 1 : members + 2]
        y = dot(jnp.concatenate(split(x), axis=0), ones)
        drive.append(y[:members] + y[members:])
    u = [apply(q, drive[q]) for q in qs]
    mean_weight = [apply(q, u[q]) for q in qs]
    trans = [
        (z[q] * jnp.sqrt(inv[q]) + mean_weight[q] * (inv[q] / (members - 1))).astype(BF16) for q in qs
    ]

    for copy in swaps:
        copy.wait()
    mine.wait()
    for q in qs:
        prior = jnp.concatenate([got[l, :, q * wide : (q + 1) * wide].astype(F32) for l in range(lags)], axis=0)
        mean = dot(prior.astype(BF16), ones) / members
        mixed = mean + dot((prior - mean).astype(BF16), diag(trans[q]))
        for l in range(lags):
            back[l, :, q * wide : (q + 1) * wide] = mixed[l * rows : (l + 1) * rows].astype(BF16)
    returns = [
        remote(back.at[peer], home.at[me], back_send.at[d], back_recv.at[d], {"lag": peer})
        for d, peer in enumerate(peers)
    ]
    for copy in returns:
        copy.start()
    mine = pltpu.make_async_copy(back.at[me], home.at[me], self_sem.at[2])
    mine.start()

    @pl.when(me == holder)
    def _():
        for d in range(lags - 1):
            spread(d).wait_send()

    mine.wait()
    for copy in returns:
        copy.wait()
    for c in range(0, cols, 2):
        at = (c % share) * members
        x = home[c // share, :, at : at + 2 * members].astype(F32)
        turned[pl.ds(c, rows, stride=cols), :] = x
        turned[pl.ds(c + 1, rows, stride=cols), :] = pltpu.roll(x, members, 1)
    for r in range(rows):
        x = turned[r * cols : (r + 1) * cols, :].T
        out_ref[r // species, r % species] = x[:members].astype(BF16)


def body(prior, obs_value, obs_weight, obs_coef, obs_column, obs_count, halo_lists, neighbours, localization):
    lags, tiles = lax.axis_size("lag"), lax.axis_size("space")
    windows, species, members, cols = prior.shape
    slots, halo, near = obs_column.shape[0], halo_lists.shape[1], neighbours.shape[0]
    share = cols // lags
    rows = windows * species
    block = pltpu.VMEM((lags, rows, share * members), BF16)
    feats = members + 16
    args = (
        prior,
        obs_value.reshape(1, slots),
        obs_weight.reshape(1, slots),
        obs_coef,
        obs_column.reshape(1, slots),
        halo_lists,
        neighbours,
        localization,
    )
    dma = pltpu.SemaphoreType.DMA
    return pl.pallas_call(
        functools.partial(kernel, tiles, lags),
        out_shape=jax.ShapeDtypeStruct(prior.shape, BF16),
        in_specs=[SMEM] + [ANY] * len(args),
        out_specs=VMEM,
        scratch_shapes=[pltpu.VMEM(x.shape, x.dtype) for x in args]
        + [
            pltpu.VMEM((species, members, cols), BF16),
            pltpu.VMEM((rows * cols, 2 * members), F32),
            block,
            block,
            block,
            block,
            pltpu.VMEM((feats, slots), BF16),
            pltpu.VMEM((2, feats, halo), BF16),
            pltpu.VMEM((2, feats, halo), BF16),
            pltpu.VMEM((cols, slots), BF16),
            pltpu.VMEM((2, slots, halo), BF16),
            pltpu.VMEM((share // PACK, 2 * halo, PACK * members), BF16),
            pltpu.VMEM((cols, 2 * near), F32),
            pltpu.VMEM((cols, 2 * near), F32),
            dma((len(args),)),
            dma((lags - 1,)),
            dma,
            dma((lags - 1,)),
            dma((lags - 1,)),
            dma((2,)),
            dma((2,)),
            dma((lags - 1,)),
            dma((lags - 1,)),
            dma((3,)),
        ],
        compiler_params=pltpu.CompilerParams(collective_id=0, has_side_effects=True),
        name="smoother",
    )(obs_count, *args)


def solution(mesh):
    return jax.shard_map(
        body,
        mesh=mesh,
        in_specs=(
            P("lag", None, None, "space"),
            P("space"),
            P("space"),
            P(None, "space"),
            P("space"),
            P("space"),
            P(None, "space"),
            P(None, "space"),
            P(None, "space"),
        ),
        out_specs=P("lag", None, None, "space"),
        check_vma=False,
    )
```

```python
import functools

import jax
import jax.numpy as jnp
from jax import lax
from jax.experimental import pallas as pl
from jax.experimental.pallas import tpu as pltpu
from jax.sharding import PartitionSpec as P

MESH = pl.DeviceIdType.MESH
F32 = jnp.float32
BF16 = jnp.bfloat16
PACK = 4
VMEM = pl.BlockSpec(memory_space=pltpu.VMEM)
ANY = pl.BlockSpec(memory_space=pl.ANY)
SMEM = pl.BlockSpec(memory_space=pltpu.SMEM)


def iota(shape, dim):
    return lax.broadcasted_iota(jnp.int32, shape, dim)


def onehot(row, depth):
    return jnp.where(row == iota((depth, row.shape[1]), 0), 1.0, 0.0).astype(BF16)


def dot(a, b):
    return jnp.dot(a, b, preferred_element_type=F32)


def split(x):
    high = x.astype(BF16)
    return high, (x - high.astype(F32)).astype(BF16)


def remote(src, dst, send_sem, recv_sem, where):
    return pltpu.make_async_remote_copy(
        src_ref=src, dst_ref=dst, send_sem=send_sem, recv_sem=recv_sem, device_id=where, device_id_type=MESH
    )


def kernel(
    tiles,
    lags,
    count_ref,
    prior_ref,
    value_ref,
    weight_ref,
    coef_ref,
    column_ref,
    lists_ref,
    table_ref,
    local_ref,
    out_ref,
    prior_v,
    value_v,
    weight_v,
    coef_v,
    column_v,
    lists_v,
    table_v,
    local_v,
    newest,
    turned,
    send,
    got,
    back,
    home,
    feat_v,
    listed,
    around,
    spread_mean,
    spread_pert,
    count_v,
    pick_v,
    list_v,
    near_v,
    tabs,
    locs,
    in_sem,
    new_send,
    new_recv,
    swap_send,
    swap_recv,
    halo_send,
    halo_recv,
    pass_send,
    pass_recv,
    count_sem,
    back_send,
    back_recv,
    self_sem,
):
    t, me = lax.axis_index("space"), lax.axis_index("lag")
    windows, species, members, cols = prior_v.shape
    rows = windows * species
    share = cols // lags
    slots, half = column_v.shape[1], lists_v.shape[1]
    halo = 2 * half
    core = lax.rem(me, 2)
    partner = me + 1 - 2 * core
    near = table_v.shape[0]
    holder = lags - 1
    below, above = t > 0, t < tiles - 1
    up, down = jnp.minimum(t + 1, tiles - 1), jnp.maximum(t - 1, 0)
    peers = [lax.rem(me + d, lags) for d in range(1, lags)]

    barrier = pltpu.get_barrier_semaphore()
    for peer in peers:
        pl.semaphore_signal(barrier, inc=1, device_id={"lag": peer}, device_id_type=MESH)

    @pl.when(above)
    def _():
        pl.semaphore_signal(barrier, inc=1, device_id={"space": up}, device_id_type=MESH)

    @pl.when(below)
    def _():
        pl.semaphore_signal(barrier, inc=1, device_id={"space": down}, device_id_type=MESH)

    pairs = [
        (prior_ref, prior_v),
        (column_ref, column_v),
        (lists_ref.at[:, pl.ds(pl.multiple_of(core * half, half), half)], lists_v),
        (coef_ref, coef_v),
        (value_ref, value_v),
        (weight_ref, weight_v),
        (table_ref, table_v),
        (local_ref, local_v),
    ]
    loads = [pltpu.make_async_copy(src, dst, in_sem.at[i]) for i, (src, dst) in enumerate(pairs)]
    loads.append(pltpu.make_async_copy(count_ref, count_v, count_sem))
    for load in loads:
        load.start()

    @pl.when(below & above)
    def _():
        pl.semaphore_wait(barrier, lags + 1)

    @pl.when(below != above)
    def _():
        pl.semaphore_wait(barrier, lags)

    def spread(d):
        return remote(prior_ref.at[windows - 1], newest, new_send.at[d], new_recv, {"lag": peers[d]})

    own = pltpu.make_async_copy(prior_ref.at[windows - 1], newest, self_sem.at[0])

    @pl.when(me == holder)
    def _():
        for d in range(lags - 1):
            spread(d).start()
        own.start()

    loads[0].wait()
    for r in range(rows):
        x = prior_v[r // species, r % species].astype(F32)
        turned[r * cols : (r + 1) * cols, :] = jnp.concatenate([x, x], axis=0).T
    low = iota((1, 2 * members), 1) < members
    for c in range(0, cols, 2):
        even = turned[pl.ds(c, rows, stride=cols), :]
        odd = turned[pl.ds(c + 1, rows, stride=cols), :]
        at = (c % share) * members
        send[c // share, :, at : at + 2 * members] = jnp.where(low, even, odd).astype(BF16)
    for load in loads[1:]:
        load.wait()
    pick_v[...] = onehot(column_v[...], cols)
    for r in range(2):
        list_v[r] = onehot(lists_v[r : r + 1, :], slots)

    @pl.when(me == holder)
    def _():
        own.wait()

    @pl.when(me != holder)
    def _():
        spread(0).wait_recv()

    pick = pick_v[...]
    hx = coef_v[0:1, :] * dot(newest[0], pick)
    for s in range(1, species):
        hx = hx + coef_v[s : s + 1, :] * dot(newest[s], pick)
    mean = jnp.sum(hx, axis=0, keepdims=True) / members
    valid = jnp.where(iota((1, slots), 1) < count_v[0], 1.0, 0.0)
    feat_v[:members] = ((hx - mean) * valid).astype(BF16)
    extra = feat_v.shape[0] - members
    row = iota((extra, slots), 0)
    info0 = weight_v[...] * valid
    info1 = (value_v[...] - mean) * valid
    feat_v[members:] = jnp.where(row == 0, info0, jnp.where(row == 1, info1, 0.0)).astype(BF16)
    feat = feat_v[...]
    for r in range(2):
        listed[r] = dot(feat, list_v[r]).astype(BF16)

    def move(r, to):
        return remote(listed.at[r], around.at[r, core], halo_send.at[r], halo_recv.at[r], {"space": to})

    def hand(r):
        half_ref = around.at[r, core]
        return remote(half_ref, half_ref, pass_send.at[r], pass_recv.at[r], {"lag": partner})

    @pl.when(above)
    def _():
        move(0, up).start()

    @pl.when(below)
    def _():
        move(1, down).start()

    @pl.when(t == 0)
    def _():
        around[0] = jnp.zeros(around.shape[1:], BF16)

    @pl.when(t == tiles - 1)
    def _():
        around[1] = jnp.zeros(around.shape[1:], BF16)

    mine = pltpu.make_async_copy(send.at[me], got.at[me], self_sem.at[1])
    mine.start()
    swaps = [
        remote(send.at[peer], got.at[me], swap_send.at[d], swap_recv.at[d], {"lag": peer})
        for d, peer in enumerate(peers)
    ]
    for copy in swaps:
        copy.start()

    x = table_v[...].astype(F32)
    tabs[...] = jnp.concatenate([x, x], axis=0).T
    x = local_v[...]
    locs[...] = jnp.concatenate([x, x], axis=0).T
    start = pl.multiple_of(me * share, share)
    low = iota((1, 2 * near), 1) < near
    groups = share // PACK
    wide = PACK * members
    qs = range(groups)

    def row_of(ref, q):
        parts = []
        for m in range(0, PACK, 2):
            c = start + q * PACK + m
            parts.append(jnp.where(low, ref[pl.ds(c, 1), :], ref[pl.ds(c + 1, 1), :]))
        return jnp.concatenate(parts, axis=1)

    lane = iota((members, wide), 1)
    masks = [jnp.where(lane // members == m, 1.0, 0.0).astype(BF16) for m in range(PACK)]
    ones = jnp.concatenate(masks, axis=0)
    eye = jnp.where(lane % members == iota((members, wide), 0), 1.0, 0.0)

    def diag(x):
        return jnp.concatenate([x * mask for mask in masks], axis=0)

    local = [row_of(locs, q) for q in qs]
    inner = []
    for q in qs:
        table = row_of(tabs, q).astype(jnp.int32)
        inner.append(dot(feat, onehot(table, slots)))
        near_v[q] = onehot(table - slots, 2 * halo)

    for copy in swaps:
        copy.wait()
    mine.wait()
    for q in qs:
        at = slice(q * wide, (q + 1) * wide)
        values = jnp.concatenate([got[l, :, at].astype(F32) for l in range(lags)], axis=0)
        mean = dot(values.astype(BF16), ones) / members
        spread_mean[:, at] = mean
        spread_pert[:, at] = (values - mean).astype(BF16)

    @pl.when(above)
    def _():
        move(1, up).wait_recv()
        hand(1).start()

    @pl.when(below)
    def _():
        move(0, down).wait_recv()
        hand(0).start()

    def part(q, h):
        y = None
        for r in range(2):
            rows_at = pl.ds(pl.multiple_of((2 * r + h) * half, half), half)
            term = dot(around[r, h], near_v[q, rows_at])
            y = term if y is None else y + term
        return y

    inner = [inner[q] + part(q, core) for q in qs]

    @pl.when(above)
    def _():
        move(0, up).wait_send()
        hand(1).wait()

    @pl.when(below)
    def _():
        move(1, down).wait_send()
        hand(0).wait()

    def group_sum(x):
        high, _ = split(x)
        mid, last = split(x - high.astype(F32))
        count = x.shape[0]
        y = dot(jnp.concatenate([high.astype(F32), mid.astype(F32), last.astype(F32)], axis=0).astype(BF16), ones)
        return y[:count] + y[count : 2 * count] + y[2 * count :]

    def solve(qs):
        picked = {q: inner[q] + part(q, 1 - core) for q in qs}
        gathered = {q: picked[q][:members] for q in qs}
        weighted = {q: (gathered[q] * (local[q] * picked[q][members : members + 1])).astype(BF16) for q in qs}
        gram = {
            q: lax.dot_general(
                gathered[q].astype(BF16), diag(weighted[q]), (((1,), (1,)), ((), ())), preferred_element_type=F32
            )
            for q in qs
        }
        matrix = {q: eye + gram[q] / (members - 1) for q in qs}
        total = [jnp.sum(matrix[q] * matrix[q], axis=0, keepdims=True) for q in qs]
        root = lax.rsqrt(group_sum(jnp.concatenate(total, axis=0)))
        inv = {q: root[i : i + 1] for i, q in enumerate(qs)}
        a = {q: matrix[q] * inv[q] for q in qs}
        ab = {q: a[q].astype(BF16) for q in qs}
        p = {q: dot(ab[q], diag(ab[q])) for q in qs}
        z = {
            q: 2.25 * eye
            - 2.4375 * a[q]
            + 1.6875 * p[q]
            + dot((0.0625 * p[q] - 0.5625 * a[q]).astype(BF16), diag(p[q].astype(BF16)))
            for q in qs
        }
        zs = {q: jnp.concatenate(split(z[q]), axis=0) for q in qs}

        def apply(q, x):
            high, small = split(x)
            y = dot(zs[q], diag(high))
            return y[:members] + y[members:] + dot(zs[q][:members], diag(small))

        drive = {}
        for q in qs:
            x = weighted[q].astype(F32) * picked[q][members + 1 : members + 2]
            y = dot(jnp.concatenate(split(x), axis=0), ones)
            drive[q] = y[:members] + y[members:]
        u = {q: apply(q, drive[q]) for q in qs}
        mean_weight = {q: apply(q, u[q]) for q in qs}
        for q in qs:
            trans = (z[q] * jnp.sqrt(inv[q]) + mean_weight[q] * (inv[q] / (members - 1))).astype(BF16)
            at = slice(q * wide, (q + 1) * wide)
            mixed = spread_mean[:, at] + dot(spread_pert[:, at], diag(trans))
            for l in range(lags):
                back[l, :, at] = mixed[l * rows : (l + 1) * rows].astype(BF16)

    returns = []
    batch = -(-groups // 2)
    for b in range(2):
        first, last = b * batch, min(groups, (b + 1) * batch)
        if first >= last:
            continue
        solve(range(first, last))
        lanes = pl.ds(first * wide, (last - first) * wide)
        for d, peer in enumerate(peers):
            copy = remote(
                back.at[peer, :, lanes], home.at[me, :, lanes], back_send.at[b, d], back_recv.at[b, d], {"lag": peer}
            )
            copy.start()
            returns.append(copy)
    mine = pltpu.make_async_copy(back.at[me], home.at[me], self_sem.at[2])
    mine.start()

    @pl.when(me == holder)
    def _():
        for d in range(lags - 1):
            spread(d).wait_send()

    mine.wait()
    for copy in returns:
        copy.wait()
    for c in range(0, cols, 2):
        at = (c % share) * members
        x = home[c // share, :, at : at + 2 * members].astype(F32)
        turned[pl.ds(c, rows, stride=cols), :] = x
        turned[pl.ds(c + 1, rows, stride=cols), :] = pltpu.roll(x, members, 1)
    for r in range(rows):
        x = turned[r * cols : (r + 1) * cols, :].T
        out_ref[r // species, r % species] = x[:members].astype(BF16)


def body(prior, obs_value, obs_weight, obs_coef, obs_column, obs_count, halo_lists, neighbours, localization):
    lags, tiles = lax.axis_size("lag"), lax.axis_size("space")
    windows, species, members, cols = prior.shape
    slots, halo, near = obs_column.shape[0], halo_lists.shape[1], neighbours.shape[0]
    share = cols // lags
    rows = windows * species
    block = pltpu.VMEM((lags, rows, share * members), BF16)
    feats = members + 8
    args = (
        prior,
        obs_value.reshape(1, slots),
        obs_weight.reshape(1, slots),
        obs_coef,
        obs_column.reshape(1, slots),
        halo_lists,
        neighbours,
        localization,
    )
    dma = pltpu.SemaphoreType.DMA
    return pl.pallas_call(
        functools.partial(kernel, tiles, lags),
        out_shape=jax.ShapeDtypeStruct(prior.shape, BF16),
        in_specs=[ANY] * (1 + len(args)),
        out_specs=VMEM,
        scratch_shapes=[
            pltpu.VMEM((2, halo // 2) if x is halo_lists else x.shape, x.dtype) for x in args
        ]
        + [
            pltpu.VMEM((species, members, cols), BF16),
            pltpu.VMEM((rows * cols, 2 * members), F32),
            block,
            block,
            block,
            block,
            pltpu.VMEM((feats, slots), BF16),
            pltpu.VMEM((2, feats, halo // 2), BF16),
            pltpu.VMEM((2, 2, feats, halo // 2), BF16),
            pltpu.VMEM((lags * rows, share * members), F32),
            pltpu.VMEM((lags * rows, share * members), BF16),
            pltpu.SMEM((1,), jnp.int32),
            pltpu.VMEM((cols, slots), BF16),
            pltpu.VMEM((2, slots, halo // 2), BF16),
            pltpu.VMEM((share // PACK, 2 * halo, PACK * members), BF16),
            pltpu.VMEM((cols, 2 * near), F32),
            pltpu.VMEM((cols, 2 * near), F32),
            dma((len(args),)),
            dma((lags - 1,)),
            dma,
            dma((lags - 1,)),
            dma((lags - 1,)),
            dma((2,)),
            dma((2,)),
            dma((2,)),
            dma((2,)),
            dma,
            dma((2, lags - 1)),
            dma((2, lags - 1)),
            dma((3,)),
        ],
        compiler_params=pltpu.CompilerParams(collective_id=0, has_side_effects=True),
        name="smoother",
    )(obs_count, *args)


def solution(mesh):
    return jax.shard_map(
        body,
        mesh=mesh,
        in_specs=(
            P("lag", None, None, "space"),
            P("space"),
            P("space"),
            P(None, "space"),
            P("space"),
            P("space"),
            P(None, "space"),
            P(None, "space"),
            P(None, "space"),
        ),
        out_specs=P("lag", None, None, "space"),
        check_vma=False,
    )
```

```python
import functools

import jax
import jax.numpy as jnp
from jax import lax
from jax.experimental import pallas as pl
from jax.experimental.pallas import tpu as pltpu
from jax.sharding import PartitionSpec as P

MESH = pl.DeviceIdType.MESH
F32 = jnp.float32
BF16 = jnp.bfloat16
PACK = 4
VMEM = pl.BlockSpec(memory_space=pltpu.VMEM)
ANY = pl.BlockSpec(memory_space=pl.ANY)
SMEM = pl.BlockSpec(memory_space=pltpu.SMEM)


def iota(shape, dim):
    return lax.broadcasted_iota(jnp.int32, shape, dim)


def onehot(row, depth):
    return jnp.where(row == iota((depth, row.shape[1]), 0), 1.0, 0.0).astype(BF16)


def dot(a, b):
    return jnp.dot(a, b, preferred_element_type=F32)


def split(x):
    high = x.astype(BF16)
    return high, (x - high.astype(F32)).astype(BF16)


def remote(src, dst, send_sem, recv_sem, where):
    return pltpu.make_async_remote_copy(
        src_ref=src, dst_ref=dst, send_sem=send_sem, recv_sem=recv_sem, device_id=where, device_id_type=MESH
    )


def kernel(
    tiles,
    lags,
    count_ref,
    prior_ref,
    value_ref,
    weight_ref,
    coef_ref,
    column_ref,
    lists_ref,
    table_ref,
    local_ref,
    home,
    prior_v,
    value_v,
    weight_v,
    coef_v,
    column_v,
    lists_v,
    table_v,
    local_v,
    newest,
    turned,
    send,
    got,
    back,
    feat_v,
    listed,
    around,
    spread_mean,
    spread_pert,
    count_v,
    pick_v,
    list_v,
    near_v,
    tabs,
    locs,
    in_sem,
    new_send,
    new_recv,
    swap_send,
    swap_recv,
    halo_send,
    halo_recv,
    pass_send,
    pass_recv,
    count_sem,
    back_send,
    back_recv,
    self_sem,
):
    t, me = lax.axis_index("space"), lax.axis_index("lag")
    windows, species, members, cols = prior_v.shape
    rows = windows * species
    share = cols // lags
    slots, half = column_v.shape[1], lists_v.shape[1]
    halo = 2 * half
    core = lax.rem(me, 2)
    partner = me + 1 - 2 * core
    near = table_v.shape[0]
    holder = lags - 1
    below, above = t > 0, t < tiles - 1
    up, down = jnp.minimum(t + 1, tiles - 1), jnp.maximum(t - 1, 0)
    peers = [lax.rem(me + d, lags) for d in range(1, lags)]

    barrier = pltpu.get_barrier_semaphore()
    for peer in peers:
        pl.semaphore_signal(barrier, inc=1, device_id={"lag": peer}, device_id_type=MESH)

    @pl.when(above)
    def _():
        pl.semaphore_signal(barrier, inc=1, device_id={"space": up}, device_id_type=MESH)

    @pl.when(below)
    def _():
        pl.semaphore_signal(barrier, inc=1, device_id={"space": down}, device_id_type=MESH)

    pairs = [
        (prior_ref, prior_v),
        (column_ref, column_v),
        (lists_ref.at[:, pl.ds(pl.multiple_of(core * half, half), half)], lists_v),
        (coef_ref, coef_v),
        (value_ref, value_v),
        (weight_ref, weight_v),
        (table_ref, table_v),
        (local_ref, local_v),
    ]
    loads = [pltpu.make_async_copy(src, dst, in_sem.at[i]) for i, (src, dst) in enumerate(pairs)]
    loads.append(pltpu.make_async_copy(count_ref, count_v, count_sem))
    for load in loads:
        load.start()

    @pl.when(below & above)
    def _():
        pl.semaphore_wait(barrier, lags + 1)

    @pl.when(below != above)
    def _():
        pl.semaphore_wait(barrier, lags)

    def spread(d):
        return remote(prior_ref.at[windows - 1], newest, new_send.at[d], new_recv, {"lag": peers[d]})

    own = pltpu.make_async_copy(prior_ref.at[windows - 1], newest, self_sem.at[0])

    @pl.when(me == holder)
    def _():
        for d in range(lags - 1):
            spread(d).start()
        own.start()

    loads[0].wait()
    for r in range(rows):
        x = prior_v[r // species, r % species].astype(F32)
        turned[r * cols : (r + 1) * cols, :] = jnp.concatenate([x, x], axis=0).T
    low = iota((1, 2 * members), 1) < members
    for c in range(0, cols, 2):
        even = turned[pl.ds(c, rows, stride=cols), :]
        odd = turned[pl.ds(c + 1, rows, stride=cols), :]
        at = (c % share) * members
        send[c // share, :, at : at + 2 * members] = jnp.where(low, even, odd).astype(BF16)
    for load in loads[1:]:
        load.wait()
    pick_v[...] = onehot(column_v[...], cols)
    for r in range(2):
        list_v[r] = onehot(lists_v[r : r + 1, :], slots)

    @pl.when(me == holder)
    def _():
        own.wait()

    @pl.when(me != holder)
    def _():
        spread(0).wait_recv()

    pick = pick_v[...]
    hx = coef_v[0:1, :] * dot(newest[0], pick)
    for s in range(1, species):
        hx = hx + coef_v[s : s + 1, :] * dot(newest[s], pick)
    mean = jnp.sum(hx, axis=0, keepdims=True) / members
    valid = jnp.where(iota((1, slots), 1) < count_v[0], 1.0, 0.0)
    feat_v[:members] = ((hx - mean) * valid).astype(BF16)
    extra = feat_v.shape[0] - members
    row = iota((extra, slots), 0)
    info0 = weight_v[...] * valid
    info1 = (value_v[...] - mean) * valid
    feat_v[members:] = jnp.where(row == 0, info0, jnp.where(row == 1, info1, 0.0)).astype(BF16)
    feat = feat_v[...]
    for r in range(2):
        listed[r] = dot(feat, list_v[r]).astype(BF16)

    def move(r, to):
        return remote(listed.at[r], around.at[r, core], halo_send.at[r], halo_recv.at[r], {"space": to})

    def hand(r):
        half_ref = around.at[r, core]
        return remote(half_ref, half_ref, pass_send.at[r], pass_recv.at[r], {"lag": partner})

    @pl.when(above)
    def _():
        move(0, up).start()

    @pl.when(below)
    def _():
        move(1, down).start()

    @pl.when(t == 0)
    def _():
        around[0] = jnp.zeros(around.shape[1:], BF16)

    @pl.when(t == tiles - 1)
    def _():
        around[1] = jnp.zeros(around.shape[1:], BF16)

    mine = pltpu.make_async_copy(send.at[me], got.at[me], self_sem.at[1])
    mine.start()
    swaps = [
        remote(send.at[peer], got.at[me], swap_send.at[d], swap_recv.at[d], {"lag": peer})
        for d, peer in enumerate(peers)
    ]
    for copy in swaps:
        copy.start()

    x = table_v[...].astype(F32)
    tabs[...] = jnp.concatenate([x, x], axis=0).T
    x = local_v[...]
    locs[...] = jnp.concatenate([x, x], axis=0).T
    start = pl.multiple_of(me * share, share)
    low = iota((1, 2 * near), 1) < near
    groups = share // PACK
    wide = PACK * members
    qs = range(groups)

    def row_of(ref, q):
        parts = []
        for m in range(0, PACK, 2):
            c = start + q * PACK + m
            parts.append(jnp.where(low, ref[pl.ds(c, 1), :], ref[pl.ds(c + 1, 1), :]))
        return jnp.concatenate(parts, axis=1)

    lane = iota((members, wide), 1)
    masks = [jnp.where(lane // members == m, 1.0, 0.0).astype(BF16) for m in range(PACK)]
    ones = jnp.concatenate(masks, axis=0)
    eye = jnp.where(lane % members == iota((members, wide), 0), 1.0, 0.0)

    def diag(x):
        return jnp.concatenate([x * mask for mask in masks], axis=0)

    local = [row_of(locs, q) for q in qs]
    inner = []
    for q in qs:
        table = row_of(tabs, q).astype(jnp.int32)
        inner.append(dot(feat, onehot(table, slots)))
        near_v[q] = onehot(table - slots, 2 * halo)

    for copy in swaps:
        copy.wait()
    mine.wait()
    for q in qs:
        at = slice(q * wide, (q + 1) * wide)
        values = jnp.concatenate([got[l, :, at].astype(F32) for l in range(lags)], axis=0)
        mean = dot(values.astype(BF16), ones) / members
        spread_mean[:, at] = mean
        spread_pert[:, at] = (values - mean).astype(BF16)

    @pl.when(above)
    def _():
        move(1, up).wait_recv()
        hand(1).start()

    @pl.when(below)
    def _():
        move(0, down).wait_recv()
        hand(0).start()

    def part(q, h):
        y = None
        for r in range(2):
            rows_at = pl.ds(pl.multiple_of((2 * r + h) * half, half), half)
            term = dot(around[r, h], near_v[q, rows_at])
            y = term if y is None else y + term
        return y

    inner = [inner[q] + part(q, core) for q in qs]

    @pl.when(above)
    def _():
        move(0, up).wait_send()
        hand(1).wait()

    @pl.when(below)
    def _():
        move(1, down).wait_send()
        hand(0).wait()

    def group_sum(x):
        high, _ = split(x)
        mid, last = split(x - high.astype(F32))
        count = x.shape[0]
        y = dot(jnp.concatenate([high.astype(F32), mid.astype(F32), last.astype(F32)], axis=0).astype(BF16), ones)
        return y[:count] + y[count : 2 * count] + y[2 * count :]

    def solve(qs):
        picked = {q: inner[q] + part(q, 1 - core) for q in qs}
        gathered = {q: picked[q][:members] for q in qs}
        weighted = {q: (gathered[q] * (local[q] * picked[q][members : members + 1])).astype(BF16) for q in qs}
        gram = {
            q: lax.dot_general(
                gathered[q].astype(BF16), diag(weighted[q]), (((1,), (1,)), ((), ())), preferred_element_type=F32
            )
            for q in qs
        }
        matrix = {q: eye + gram[q] / (members - 1) for q in qs}
        total = [jnp.sum(matrix[q] * matrix[q], axis=0, keepdims=True) for q in qs]
        root = lax.rsqrt(group_sum(jnp.concatenate(total, axis=0)))
        inv = {q: root[i : i + 1] for i, q in enumerate(qs)}
        a = {q: matrix[q] * inv[q] for q in qs}
        ab = {q: a[q].astype(BF16) for q in qs}
        p = {q: dot(ab[q], diag(ab[q])) for q in qs}
        z = {
            q: 2.25 * eye
            - 2.4375 * a[q]
            + 1.6875 * p[q]
            + dot((0.0625 * p[q] - 0.5625 * a[q]).astype(BF16), diag(p[q].astype(BF16)))
            for q in qs
        }
        zs = {q: jnp.concatenate(split(z[q]), axis=0) for q in qs}

        def apply(q, x):
            high, small = split(x)
            y = dot(zs[q], diag(high))
            return y[:members] + y[members:] + dot(zs[q][:members], diag(small))

        drive = {}
        for q in qs:
            x = weighted[q].astype(F32) * picked[q][members + 1 : members + 2]
            y = dot(jnp.concatenate(split(x), axis=0), ones)
            drive[q] = y[:members] + y[members:]
        u = {q: apply(q, drive[q]) for q in qs}
        mean_weight = {q: apply(q, u[q]) for q in qs}
        for q in qs:
            trans = (z[q] * jnp.sqrt(inv[q]) + mean_weight[q] * (inv[q] / (members - 1))).astype(BF16)
            at = slice(q * wide, (q + 1) * wide)
            mixed = spread_mean[:, at] + dot(spread_pert[:, at], diag(trans))
            for l in range(lags):
                back[l, :, at] = mixed[l * rows : (l + 1) * rows].astype(BF16)

    returns = []
    batch = -(-groups // 2)
    for b in range(2):
        first, last = b * batch, min(groups, (b + 1) * batch)
        if first >= last:
            continue
        solve(range(first, last))
        lanes = pl.ds(first * wide, (last - first) * wide)
        for d, peer in enumerate(peers):
            copy = remote(
                back.at[peer, :, lanes], home.at[me, :, lanes], back_send.at[b, d], back_recv.at[b, d], {"lag": peer}
            )
            copy.start()
            returns.append(copy)
    mine = pltpu.make_async_copy(back.at[me], home.at[me], self_sem.at[2])
    mine.start()

    @pl.when(me == holder)
    def _():
        for d in range(lags - 1):
            spread(d).wait_send()

    mine.wait()
    for copy in returns:
        copy.wait()


def restore_kernel(got_ref, out_ref, turned):
    windows, species, members, cols = out_ref.shape
    rows = windows * species
    share = cols // got_ref.shape[0]
    for c in range(0, cols, 2):
        at = (c % share) * members
        x = got_ref[c // share, :, at : at + 2 * members].astype(F32)
        turned[pl.ds(c, rows, stride=cols), :] = x
        turned[pl.ds(c + 1, rows, stride=cols), :] = pltpu.roll(x, members, 1)
    for r in range(rows):
        x = turned[r * cols : (r + 1) * cols, :].T
        out_ref[r // species, r % species] = x[:members].astype(BF16)


def body(prior, obs_value, obs_weight, obs_coef, obs_column, obs_count, halo_lists, neighbours, localization):
    lags, tiles = lax.axis_size("lag"), lax.axis_size("space")
    windows, species, members, cols = prior.shape
    slots, halo, near = obs_column.shape[0], halo_lists.shape[1], neighbours.shape[0]
    share = cols // lags
    rows = windows * species
    block = pltpu.VMEM((lags, rows, share * members), BF16)
    feats = members + 8
    args = (
        prior,
        obs_value.reshape(1, slots),
        obs_weight.reshape(1, slots),
        obs_coef,
        obs_column.reshape(1, slots),
        halo_lists,
        neighbours,
        localization,
    )
    dma = pltpu.SemaphoreType.DMA
    home = pl.pallas_call(
        functools.partial(kernel, tiles, lags),
        out_shape=jax.ShapeDtypeStruct((lags, rows, share * members), BF16),
        in_specs=[ANY] * (1 + len(args)),
        out_specs=ANY,
        scratch_shapes=[
            pltpu.VMEM((2, halo // 2) if x is halo_lists else x.shape, x.dtype) for x in args
        ]
        + [
            pltpu.VMEM((species, members, cols), BF16),
            pltpu.VMEM((rows * cols, 2 * members), F32),
            block,
            block,
            block,
            pltpu.VMEM((feats, slots), BF16),
            pltpu.VMEM((2, feats, halo // 2), BF16),
            pltpu.VMEM((2, 2, feats, halo // 2), BF16),
            pltpu.VMEM((lags * rows, share * members), F32),
            pltpu.VMEM((lags * rows, share * members), BF16),
            pltpu.SMEM((1,), jnp.int32),
            pltpu.VMEM((cols, slots), BF16),
            pltpu.VMEM((2, slots, halo // 2), BF16),
            pltpu.VMEM((share // PACK, 2 * halo, PACK * members), BF16),
            pltpu.VMEM((cols, 2 * near), F32),
            pltpu.VMEM((cols, 2 * near), F32),
            dma((len(args),)),
            dma((lags - 1,)),
            dma,
            dma((lags - 1,)),
            dma((lags - 1,)),
            dma((2,)),
            dma((2,)),
            dma((2,)),
            dma((2,)),
            dma,
            dma((2, lags - 1)),
            dma((2, lags - 1)),
            dma((3,)),
        ],
        compiler_params=pltpu.CompilerParams(collective_id=0, has_side_effects=True),
        name="smoother",
    )(obs_count, *args)
    return pl.pallas_call(
        restore_kernel,
        out_shape=jax.ShapeDtypeStruct(prior.shape, BF16),
        in_specs=[VMEM],
        out_specs=VMEM,
        scratch_shapes=[pltpu.VMEM((rows * cols, 2 * members), F32)],
        name="restore",
    )(home)


def solution(mesh):
    return jax.shard_map(
        body,
        mesh=mesh,
        in_specs=(
            P("lag", None, None, "space"),
            P("space"),
            P("space"),
            P(None, "space"),
            P("space"),
            P("space"),
            P(None, "space"),
            P(None, "space"),
            P(None, "space"),
        ),
        out_specs=P("lag", None, None, "space"),
        check_vma=False,
    )
```
